256 devices in a mesh: gx: 4 (over x_lo, core), gy: 8 (over z), gz: 8 (over x_hi, y).
Axes of the slice: x: 4 (x_hi: 2, x_lo: 2; x = x_hi * 2 + x_lo), y: 4, z: 8, core: 2. Of those that a mesh axis runs over, the one named last changes fastest.
Arguments:
- traces: bfloat16 [2, 4, 8, 8, 512, 768], P(None, 'gx', 'gy', 'gz'), may hold values from -6 to 6
- sources: bfloat16 [2, 4, 8, 8, 512, 768], P(None, 'gx', 'gy', 'gz'), may hold values from -4 to 4
- local_ops: bfloat16 [2, 4, 8, 8, 768, 768], P(None, 'gx', 'gy', 'gz'), may hold values from -0.15625 to 0.15625
- plane_coupling: bfloat16 [4, 64, 64], P('gx'), may hold values from -0.375 to 0.375
- face_owner: int32 [4, 64], P('gx'), may hold values from 0 to 63, each once within a row
Outputs:
- new_traces: bfloat16 [2, 4, 8, 8, 512, 768], P(None, 'gx', 'gy', 'gz')
The draws below stay inside these ranges and needn't reach their ends.
Inputs may be any that keep to these rules, and one draw needn't show every extreme that they name: `face_owner`: each row is a permutation of the 64 plane positions.
All inputs are finite; a program needn't handle non-finite values.
Results may differ from the reference program's by a relative error of at most 0.0062.
Values may be sent and summed in bfloat16 or wider, within the bound.
A program may use at most 64 MiB of HBM per device.

```python
import jax
import jax.numpy as jnp
from jax import lax

W = 128
SLABS = 512
SWEEPS = 2
PLANE = 64
N_GX = 4
N_GY = 8
N_GZ = 8


def steps_of(rng, extent, cuts, low, top_value):
    def one(dim, shards_of):
        steps = jax.random.uniform(jax.random.fold_in(jax.random.fold_in(rng, 6), dim), (shards_of,), jnp.float32, low / len(cuts), top_value / len(cuts))
        return jnp.repeat(jnp.exp(steps), extent[dim] // shards_of).reshape((-1,) + (1,) * (len(extent) - dim - 1))

    loudness = one(*cuts[0])
    for cut in cuts[1:]:
        loudness = loudness * one(*cut)
    return loudness


def gaussian(stream_key, shape, spread, limit, split=(), dtype=jnp.bfloat16):
    array = spread * jax.random.normal(stream_key, shape, jnp.float32)
    if split:
        array = array * steps_of(stream_key, shape, split, -0.22, 0.18)
    return jnp.clip(array, -limit, limit).astype(dtype)


def setup_inputs(seed: int = 0) -> dict:
    keys = jax.random.split(jax.random.key(seed), 6)
    return {
        "traces": gaussian(keys[0], (2, N_GX, N_GY, N_GZ, SLABS, 6 * W), 1.0, 6.0, ((1, 4), (2, 8), (3, 8))),
        "sources": gaussian(keys[1], (2, N_GX, N_GY, N_GZ, SLABS, 6 * W), 0.5, 4.0, ((1, 4), (2, 8), (3, 8))),
        "local_ops": gaussian(keys[2], (2, N_GX, N_GY, N_GZ, 6 * W, 6 * W), (12 * W) ** -0.5, 0.15625, ((1, 4), (2, 8), (3, 8))),
        "plane_coupling": gaussian(keys[3], (N_GX, PLANE, PLANE), (4 * PLANE) ** -0.5, 0.375, ((0, 4),)),
        "face_owner": jax.vmap(lambda own: jax.random.permutation(own, PLANE))(jax.random.split(keys[4], N_GX)).reshape((N_GX, PLANE)).astype(jnp.int32),
    }


def solve_layer(layer_data):
    incoming, source_rows, operators = layer_data
    incoming = incoming.astype(jnp.float32)
    operators = operators.astype(jnp.float32)
    source_rows = source_rows.astype(jnp.float32)
    real_part = jnp.einsum('yzsc,yzcd->yzsd', incoming[0], operators[0]) - jnp.einsum('yzsc,yzcd->yzsd', incoming[1], operators[1]) + source_rows[0]
    imag_part = jnp.einsum('yzsc,yzcd->yzsd', incoming[0], operators[1]) + jnp.einsum('yzsc,yzcd->yzsd', incoming[1], operators[0]) + source_rows[1]
    return jnp.stack([real_part, imag_part]).astype(jnp.bfloat16)


def transmit(outgoing):
    face_view = outgoing.reshape(outgoing.shape[:5] + (6, W))
    moved_faces = []
    for dim_index in range(3):
        mesh_dim = 1 + dim_index
        lower_face = face_view[:, :, :, :, :, 2 * dim_index]
        upper_face = face_view[:, :, :, :, :, 2 * dim_index + 1]
        moved_faces.append(jnp.roll(upper_face, 1, axis=mesh_dim))
        moved_faces.append(jnp.roll(lower_face, -1, axis=mesh_dim))
    return jnp.stack(moved_faces, axis=5).reshape(outgoing.shape)


def couple_layer(layer_data):
    received, coupling, owners = layer_data
    picked = jnp.take(received, owners, axis=1).astype(jnp.float32)
    coupled = jnp.einsum('pq,rqsc->rpsc', coupling.astype(jnp.float32), picked)
    return (received.astype(jnp.float32) - coupled).astype(jnp.bfloat16)


def reference(traces, sources, local_ops, plane_coupling, face_owner):
    plane_size = N_GY * N_GZ
    incoming = traces
    source_view = jnp.moveaxis(sources, 1, 0)
    operator_view = jnp.moveaxis(local_ops, 1, 0)
    for sweep_step in range(SWEEPS):
        outgoing = lax.map(solve_layer, (jnp.moveaxis(incoming, 1, 0), source_view, operator_view))
        outgoing = jnp.moveaxis(outgoing, 0, 1)
        received = transmit(outgoing)
        stacked = jnp.moveaxis(received.reshape(2, N_GX, plane_size, SLABS, 6 * W), 1, 0)
        updated = lax.map(couple_layer, (stacked, plane_coupling, face_owner))
        incoming = jnp.moveaxis(updated, 0, 1).reshape(traces.shape)
    return incoming
```

```python
import functools

import jax
import jax.numpy as jnp
from jax import lax
from jax.experimental import pallas as pl
from jax.experimental.pallas import tpu as pltpu
from jax.sharding import PartitionSpec as P

SWEEPS = 2
FACES = 6
W = 128
SUB = 16
ORDER = (3, 2, 5, 4, 0, 1)
SHIFT_Y = {2: 1, 3: -1}
SHIFT_Z = {4: 1, 5: -1}
MESH = pl.DeviceIdType.MESH


def kernel(
    nx, ny, nz, slabs,
    traces, sources, ops, coupling, owners, out,
    in0, in1, in2, sent, xr, zr, kr, ur, zs, sv, bv, mi,
    load_sem, out_sem, xs_sem, xr_sem, s_sem, r_sem,
):
    i = lax.axis_index("gx")
    j = lax.axis_index("gy")
    k = lax.axis_index("gz")
    rows = 2 * slabs
    block = rows // ny
    plane = ny * nz
    incoming = (in0, in1, in2)

    for c in range(2):
        for f in range(FACES):
            pltpu.make_async_copy(
                traces.at[c, :, pl.ds(f * W, W)],
                in0.at[f, pl.ds(c * slabs, slabs), :],
                load_sem.at[0],
            ).start()
    load_ops = pltpu.make_async_copy(ops, sv, load_sem.at[1])
    load_ops.start()
    load_sources = pltpu.make_async_copy(sources, bv, load_sem.at[2])
    load_sources.start()

    barrier = pltpu.get_barrier_semaphore()
    left = lax.rem(i + nx - 1, nx)
    right = lax.rem(i + 1, nx)
    for target in (left, right):
        pl.semaphore_signal(barrier, inc=1, device_id={"gx": target}, device_id_type=MESH)
    for d in range(1, ny):
        pl.semaphore_signal(
            barrier, inc=1, device_id={"gy": lax.rem(j + d, ny)}, device_id_type=MESH
        )
    for d in range(1, nz):
        pl.semaphore_signal(
            barrier, inc=1, device_id={"gz": lax.rem(k + d, nz)}, device_id_type=MESH
        )

    def local_solve(s, f):
        w = jnp.concatenate([sv[0, :, f * W:(f + 1) * W], sv[1, :, f * W:(f + 1) * W]], axis=1)
        step = min(256, slabs)
        source = incoming[s]

        def part(t, carry):
            at = pl.multiple_of(t * step, step)
            im_at = pl.multiple_of(slabs + t * step, step)
            re = jnp.concatenate([source[g, pl.ds(at, step), :] for g in range(FACES)], axis=1)
            im = jnp.concatenate([source[g, pl.ds(im_at, step), :] for g in range(FACES)], axis=1)
            p = jnp.dot(re, w, preferred_element_type=jnp.float32)
            q = jnp.dot(im, w, preferred_element_type=jnp.float32)
            b0 = bv[0, pl.ds(at, step), f * W:(f + 1) * W].astype(jnp.float32)
            b1 = bv[1, pl.ds(at, step), f * W:(f + 1) * W].astype(jnp.float32)
            sent[s, f, pl.ds(at, step), :] = (p[:, :W] - q[:, W:] + b0).astype(jnp.bfloat16)
            sent[s, f, pl.ds(im_at, step), :] = (p[:, W:] + q[:, :W] + b1).astype(jnp.bfloat16)
            return carry

        lax.fori_loop(0, slabs // step, part, 0)

    def ring(n, body):
        def step(t, carry):
            half = (t + 1) // 2
            odd = lax.rem(t, 2)
            body(odd * half + (1 - odd) * (n - half))
            return carry

        lax.fori_loop(1, n, step, 0)

    def z_send(s, g, face):
        slot = lax.rem(j + SHIFT_Y.get(g, 0) + ny, ny)

        def one(d):
            to = lax.rem(j + d, ny)
            pltpu.make_async_remote_copy(
                src_ref=face.at[pl.ds(pl.multiple_of(to * block, block), block), :],
                dst_ref=zr.at[s, g, slot],
                send_sem=s_sem.at[s, 0, g],
                recv_sem=r_sem.at[s, 0, g],
                device_id={"gy": to},
                device_id_type=MESH,
            ).start()

        ring(ny, one)
        pltpu.make_async_copy(
            face.at[pl.ds(pl.multiple_of(j * block, block), block), :],
            zr.at[s, g, slot],
            r_sem.at[s, 0, g],
        ).start()

    def k_send(s, g):
        slot = lax.rem(k + SHIFT_Z.get(g, 0) + nz, nz)

        def one(d):
            to = lax.rem(k + d, nz)
            pltpu.make_async_remote_copy(
                src_ref=zr.at[s, g, :, pl.ds(pl.multiple_of(to * SUB, SUB), SUB), :],
                dst_ref=kr.at[s, g, slot],
                send_sem=s_sem.at[s, 1, g],
                recv_sem=r_sem.at[s, 1, g],
                device_id={"gz": to},
                device_id_type=MESH,
            ).start()

        ring(nz, one)
        pltpu.make_async_copy(
            zr.at[s, g, :, pl.ds(pl.multiple_of(k * SUB, SUB), SUB), :],
            kr.at[s, g, slot],
            r_sem.at[s, 1, g],
        ).start()

    def update(s, g):
        step = min(256, rows)
        values = kr[s, g].reshape(rows, W)

        def part(t, carry):
            at = pl.multiple_of(t * step, step)
            slots = step // (ny * SUB)
            first = t * slots
            coupled = jnp.dot(mi[pl.ds(at, step), :], values, preferred_element_type=jnp.float32)
            mine = kr[s, g, pl.ds(first, slots)].reshape(step, W).astype(jnp.float32)
            ur[s, g, pl.ds(first, slots)] = (
                (mine - coupled).astype(jnp.bfloat16).reshape(slots, ny, SUB, W)
            )
            return carry

        lax.fori_loop(0, rows // step, part, 0)

    def k_return(s, g):
        mine = pl.ds(pl.multiple_of(k * SUB, SUB), SUB)

        def one(d):
            to = lax.rem(k + d, nz)
            pltpu.make_async_remote_copy(
                src_ref=ur.at[s, g, to],
                dst_ref=zs.at[s, g, :, mine, :],
                send_sem=s_sem.at[s, 2, g],
                recv_sem=r_sem.at[s, 2, g],
                device_id={"gz": to},
                device_id_type=MESH,
            ).start()

        ring(nz, one)
        pltpu.make_async_copy(
            ur.at[s, g, k], zs.at[s, g, :, mine, :], r_sem.at[s, 2, g]
        ).start()

    def z_return(s, g):
        mine = pl.ds(pl.multiple_of(j * block, block), block)
        target = incoming[s + 1]

        def one(d):
            to = lax.rem(j + d, ny)
            pltpu.make_async_remote_copy(
                src_ref=zs.at[s, g, to],
                dst_ref=target.at[g, mine, :],
                send_sem=s_sem.at[s, 3, g],
                recv_sem=r_sem.at[s, 3, g],
                device_id={"gy": to},
                device_id_type=MESH,
            ).start()

        ring(ny, one)
        pltpu.make_async_copy(
            zs.at[s, g, j], target.at[g, mine, :], r_sem.at[s, 3, g]
        ).start()

    def arrive(sem, ref):
        pltpu.make_async_copy(ref, ref, sem).wait()

    def x_send(s, f, to, slot):
        pltpu.make_async_remote_copy(
            src_ref=sent.at[s, f],
            dst_ref=xr.at[s, slot],
            send_sem=xs_sem.at[s, slot],
            recv_sem=xr_sem.at[s, slot],
            device_id={"gx": to},
            device_id_type=MESH,
        ).start()

    def build_mixing():
        owner = jnp.broadcast_to(owners[...], (plane, plane))
        pick = (owner == lax.broadcasted_iota(jnp.int32, (plane, plane), 1)).astype(jnp.bfloat16)
        mixing = jnp.dot(coupling[...], pick, preferred_element_type=jnp.float32)
        mixing = mixing.astype(jnp.bfloat16)

        def place(index):
            point = index // SUB
            return lax.rem(point, ny) * nz + point // ny

        column = lax.broadcasted_iota(jnp.int32, (plane, rows), 1)
        spread = (lax.broadcasted_iota(jnp.int32, (plane, rows), 0) == place(column)).astype(
            jnp.bfloat16
        )
        right_part = jnp.dot(mixing, spread, preferred_element_type=jnp.float32).astype(
            jnp.bfloat16
        )
        step = min(128, rows)

        def part(t, carry):
            at = pl.multiple_of(t * step, step)
            row = lax.broadcasted_iota(jnp.int32, (step, plane), 0) + at
            choose = (place(row) == lax.broadcasted_iota(jnp.int32, (step, plane), 1)).astype(
                jnp.bfloat16
            )
            full = jnp.dot(choose, right_part, preferred_element_type=jnp.float32)
            same = lax.rem(
                lax.broadcasted_iota(jnp.int32, (step, rows), 0), SUB
            ) == lax.rem(lax.broadcasted_iota(jnp.int32, (step, rows), 1), SUB)
            mi[pl.ds(at, step), :] = jnp.where(same, full, 0.0).astype(jnp.bfloat16)
            return carry

        lax.fori_loop(0, rows // step, part, 0)

    arrive(load_sem.at[0], in0)
    load_ops.wait()
    load_sources.wait()
    pl.semaphore_wait(barrier, 2 + (ny - 1) + (nz - 1))

    for s in range(SWEEPS):
        local_solve(s, 2)
        z_send(s, 3, sent.at[s, 2])
        local_solve(s, 0)
        x_send(s, 0, left, 1)
        local_solve(s, 1)
        x_send(s, 1, right, 0)
        for g in ORDER[1:4]:
            local_solve(s, g ^ 1)
            z_send(s, g, sent.at[s, g ^ 1])
        if s == 0:
            build_mixing()
        for g in ORDER[4:]:
            arrive(xr_sem.at[s, g], xr.at[s, g])
            z_send(s, g, xr.at[s, g])
        for t in range(FACES + 2):
            if t < FACES:
                g = ORDER[t]
                arrive(r_sem.at[s, 0, g], zr.at[s, g])
                k_send(s, g)
            if 1 <= t <= FACES:
                g = ORDER[t - 1]
                arrive(r_sem.at[s, 1, g], kr.at[s, g])
                update(s, g)
                k_return(s, g)
            if t >= 2:
                g = ORDER[t - 2]
                arrive(r_sem.at[s, 2, g], zs.at[s, g])
                z_return(s, g)
        target = incoming[s + 1]
        for g in ORDER:
            arrive(r_sem.at[s, 3, g], target.at[g])
            if s == SWEEPS - 1:
                for c in range(2):
                    pltpu.make_async_copy(
                        target.at[g, pl.ds(c * slabs, slabs), :],
                        out.at[c, :, pl.ds(g * W, W)],
                        out_sem.at[g],
                    ).start()

    for s in range(SWEEPS):
        for g in range(FACES):
            arrive(s_sem.at[s, 0, g], zr.at[s, g, pl.ds(0, ny - 1)])
            arrive(s_sem.at[s, 1, g], kr.at[s, g, pl.ds(0, nz - 1)])
            arrive(s_sem.at[s, 2, g], kr.at[s, g, pl.ds(0, nz - 1)])
            arrive(s_sem.at[s, 3, g], zr.at[s, g, pl.ds(0, ny - 1)])
        for slot in range(2):
            arrive(xs_sem.at[s, slot], xr.at[s, slot])
    for g in range(FACES):
        arrive(out_sem.at[g], in2.at[g])


def on_device(nx, ny, nz, traces, sources, local_ops, plane_coupling, face_owner):
    slabs = traces.shape[4]
    columns = traces.shape[5]
    rows = 2 * slabs
    plane = ny * nz
    block = rows // ny
    bf16 = jnp.bfloat16
    hbm = pl.BlockSpec(memory_space=pl.ANY)
    vmem = pl.BlockSpec(memory_space=pltpu.VMEM)
    faces = (FACES, rows, W)
    out = pl.pallas_call(
        functools.partial(kernel, nx, ny, nz, slabs),
        out_shape=jax.ShapeDtypeStruct((2, slabs, columns), bf16),
        in_specs=[hbm, hbm, hbm, vmem, vmem],
        out_specs=hbm,
        scratch_shapes=[
            pltpu.VMEM(faces, bf16),
            pltpu.VMEM(faces, bf16),
            pltpu.VMEM(faces, bf16),
            pltpu.VMEM((SWEEPS,) + faces, bf16),
            pltpu.VMEM((SWEEPS, 2, rows, W), bf16),
            pltpu.VMEM((SWEEPS, FACES, ny, block, W), bf16),
            pltpu.VMEM((SWEEPS, FACES, nz, ny, SUB, W), bf16),
            pltpu.VMEM((SWEEPS, FACES, nz, ny, SUB, W), bf16),
            pltpu.VMEM((SWEEPS, FACES, ny, block, W), bf16),
            pltpu.VMEM((2, columns, columns), bf16),
            pltpu.VMEM((2, slabs, columns), bf16),
            pltpu.VMEM((rows, rows), bf16),
            pltpu.SemaphoreType.DMA((3,)),
            pltpu.SemaphoreType.DMA((FACES,)),
            pltpu.SemaphoreType.DMA((SWEEPS, 2)),
            pltpu.SemaphoreType.DMA((SWEEPS, 2)),
            pltpu.SemaphoreType.DMA((SWEEPS, 4, FACES)),
            pltpu.SemaphoreType.DMA((SWEEPS, 4, FACES)),
        ],
        compiler_params=pltpu.CompilerParams(
            collective_id=0, has_side_effects=True, vmem_limit_bytes=60 << 20
        ),
    )(
        traces.reshape(2, slabs, columns),
        sources.reshape(2, slabs, columns),
        local_ops.reshape(2, columns, columns),
        plane_coupling.reshape(plane, plane),
        face_owner.reshape(plane, 1),
    )
    return out.reshape(traces.shape)


def solution(mesh):
    placed = (
        P(None, "gx", "gy", "gz", None, None),
        P(None, "gx", "gy", "gz", None, None),
        P(None, "gx", "gy", "gz", None, None),
        P("gx", None, None),
        P("gx", None),
    )
    sizes = tuple(mesh.shape[axis] for axis in ("gx", "gy", "gz"))
    return jax.shard_map(
        functools.partial(on_device, *sizes),
        mesh=mesh,
        in_specs=placed,
        out_specs=P(None, "gx", "gy", "gz", None, None),
        check_vma=False,
    )
```

```python
import functools

import jax
import jax.numpy as jnp
from jax import lax
from jax.experimental import pallas as pl
from jax.experimental.pallas import tpu as pltpu
from jax.sharding import PartitionSpec as P

SWEEPS = 2
FACES = 6
W = 128
SUB = 16
ORDER = (3, 2, 5, 4, 0, 1)
SHIFT_Y = {2: 1, 3: -1}
SHIFT_Z = {4: 1, 5: -1}
MESH = pl.DeviceIdType.MESH


def kernel(
    nx, ny, nz, slabs,
    traces, sources, ops, coupling_hbm, owners_hbm, out,
    in0, in1, sent, xr, zr, kr, ur, zs, sv, bv, mi, coupling, owners,
    load_sem, xs_sem, xr_sem, s_sem, r_sem,
):
    i = lax.axis_index("gx")
    j = lax.axis_index("gy")
    k = lax.axis_index("gz")
    rows = 2 * slabs
    block = rows // ny
    plane = ny * nz
    incoming = (in0, in1)

    for c in range(2):
        for f in range(FACES):
            pltpu.make_async_copy(
                traces.at[c, :, pl.ds(f * W, W)],
                in0.at[f, pl.ds(c * slabs, slabs), :],
                load_sem.at[0],
            ).start()
    tables = [
        pltpu.make_async_copy(coupling_hbm, coupling, load_sem.at[7]),
        pltpu.make_async_copy(owners_hbm, owners, load_sem.at[8]),
    ]
    loads = []
    for n, columns in enumerate((pl.ds(2 * W, W), pl.ds(0, 2 * W), pl.ds(3 * W, 3 * W))):
        load = [
            pltpu.make_async_copy(ops.at[:, :, columns], sv.at[:, :, columns], load_sem.at[1 + 2 * n]),
            pltpu.make_async_copy(
                sources.at[:, :, columns], bv.at[:, :, columns], load_sem.at[2 + 2 * n]
            ),
        ]
        for copy in load:
            copy.start()
        loads.append(load)
    for copy in tables:
        copy.start()

    barrier = pltpu.get_barrier_semaphore()
    left = lax.rem(i + nx - 1, nx)
    right = lax.rem(i + 1, nx)
    for target in (left, right):
        pl.semaphore_signal(barrier, inc=1, device_id={"gx": target}, device_id_type=MESH)
    for d in range(1, ny):
        pl.semaphore_signal(
            barrier, inc=1, device_id={"gy": lax.rem(j + d, ny)}, device_id_type=MESH
        )
    for d in range(1, nz):
        pl.semaphore_signal(
            barrier, inc=1, device_id={"gz": lax.rem(k + d, nz)}, device_id_type=MESH
        )

    def local_solve(s, f):
        w = jnp.concatenate([sv[0, :, f * W:(f + 1) * W], sv[1, :, f * W:(f + 1) * W]], axis=1)
        step = min(256, slabs)
        source = incoming[s]

        def part(t, carry):
            at = pl.multiple_of(t * step, step)
            im_at = pl.multiple_of(slabs + t * step, step)
            re = jnp.concatenate([source[g, pl.ds(at, step), :] for g in range(FACES)], axis=1)
            im = jnp.concatenate([source[g, pl.ds(im_at, step), :] for g in range(FACES)], axis=1)
            p = jnp.dot(re, w, preferred_element_type=jnp.float32)
            q = jnp.dot(im, w, preferred_element_type=jnp.float32)
            b0 = bv[0, pl.ds(at, step), f * W:(f + 1) * W].astype(jnp.float32)
            b1 = bv[1, pl.ds(at, step), f * W:(f + 1) * W].astype(jnp.float32)
            sent[s, f, pl.ds(at, step), :] = (p[:, :W] - q[:, W:] + b0).astype(jnp.bfloat16)
            sent[s, f, pl.ds(im_at, step), :] = (p[:, W:] + q[:, :W] + b1).astype(jnp.bfloat16)
            return carry

        lax.fori_loop(0, slabs // step, part, 0)

    def ring(n, body):
        def step(t, carry):
            half = (t + 1) // 2
            odd = lax.rem(t, 2)
            body(odd * half + (1 - odd) * (n - half))
            return carry

        lax.fori_loop(1, n, step, 0)

    def z_send(s, g, face):
        slot = lax.rem(j + SHIFT_Y.get(g, 0) + ny, ny)

        def one(d):
            to = lax.rem(j + d, ny)
            pltpu.make_async_remote_copy(
                src_ref=face.at[pl.ds(pl.multiple_of(to * block, block), block), :],
                dst_ref=zr.at[s, g, slot],
                send_sem=s_sem.at[s, 0, g],
                recv_sem=r_sem.at[s, 0, g],
                device_id={"gy": to},
                device_id_type=MESH,
            ).start()

        ring(ny, one)
        pltpu.make_async_copy(
            face.at[pl.ds(pl.multiple_of(j * block, block), block), :],
            zr.at[s, g, slot],
            r_sem.at[s, 0, g],
        ).start()

    def k_send(s, g):
        slot = lax.rem(k + SHIFT_Z.get(g, 0) + nz, nz)

        def one(d):
            to = lax.rem(k + d, nz)
            pltpu.make_async_remote_copy(
                src_ref=zr.at[s, g, :, pl.ds(pl.multiple_of(to * SUB, SUB), SUB), :],
                dst_ref=kr.at[s, g, slot],
                send_sem=s_sem.at[s, 1, g],
                recv_sem=r_sem.at[s, 1, g],
                device_id={"gz": to},
                device_id_type=MESH,
            ).start()

        ring(nz, one)
        pltpu.make_async_copy(
            zr.at[s, g, :, pl.ds(pl.multiple_of(k * SUB, SUB), SUB), :],
            kr.at[s, g, slot],
            r_sem.at[s, 1, g],
        ).start()

    def update(s, g):
        step = min(256, rows)
        values = kr[s, g].reshape(rows, W)

        def part(t, carry):
            at = pl.multiple_of(t * step, step)
            slots = step // (ny * SUB)
            first = t * slots
            coupled = jnp.dot(mi[pl.ds(at, step), :], values, preferred_element_type=jnp.float32)
            mine = kr[s, g, pl.ds(first, slots)].reshape(step, W).astype(jnp.float32)
            ur[s, g, pl.ds(first, slots)] = (
                (mine - coupled).astype(jnp.bfloat16).reshape(slots, ny, SUB, W)
            )
            return carry

        lax.fori_loop(0, rows // step, part, 0)

    def k_return(s, g):
        mine = pl.ds(pl.multiple_of(k * SUB, SUB), SUB)

        def one(d):
            to = lax.rem(k + d, nz)
            pltpu.make_async_remote_copy(
                src_ref=ur.at[s, g, to],
                dst_ref=zs.at[s, g, :, mine, :],
                send_sem=s_sem.at[s, 2, g],
                recv_sem=r_sem.at[s, 2, g],
                device_id={"gz": to},
                device_id_type=MESH,
            ).start()

        ring(nz, one)
        pltpu.make_async_copy(
            ur.at[s, g, k], zs.at[s, g, :, mine, :], r_sem.at[s, 2, g]
        ).start()

    def z_return(s, g):
        if s == SWEEPS - 1:
            part = slabs // block
            rows_at = pl.multiple_of(lax.rem(j, part) * block, block)
            home = out.at[j // part, pl.ds(rows_at, block), g * W:(g + 1) * W]
        else:
            rows_at = pl.multiple_of(j * block, block)
            home = incoming[s + 1].at[g, pl.ds(rows_at, block), :]

        def one(d):
            to = lax.rem(j + d, ny)
            pltpu.make_async_remote_copy(
                src_ref=zs.at[s, g, to],
                dst_ref=home,
                send_sem=s_sem.at[s, 3, g],
                recv_sem=r_sem.at[s, 3, g],
                device_id={"gy": to},
                device_id_type=MESH,
            ).start()

        ring(ny, one)
        pltpu.make_async_copy(
            zs.at[s, g, j], home, r_sem.at[s, 3, g]
        ).start()

    def arrive(sem, ref):
        pltpu.make_async_copy(ref, ref, sem).wait()

    def x_send(s, f, to, slot):
        pltpu.make_async_remote_copy(
            src_ref=sent.at[s, f],
            dst_ref=xr.at[s, slot],
            send_sem=xs_sem.at[s, slot],
            recv_sem=xr_sem.at[s, slot],
            device_id={"gx": to},
            device_id_type=MESH,
        ).start()

    def build_mixing():
        owner = jnp.broadcast_to(owners[...], (plane, plane))
        pick = (owner == lax.broadcasted_iota(jnp.int32, (plane, plane), 0)).astype(jnp.bfloat16)
        mixing = lax.dot_general(
            coupling[...], pick, (((1,), (1,)), ((), ())), preferred_element_type=jnp.float32
        )
        mixing = mixing.astype(jnp.bfloat16)

        def place(index):
            point = index // SUB
            return lax.rem(point, ny) * nz + point // ny

        column = lax.broadcasted_iota(jnp.int32, (plane, rows), 1)
        spread = (lax.broadcasted_iota(jnp.int32, (plane, rows), 0) == place(column)).astype(
            jnp.bfloat16
        )
        right_part = jnp.dot(mixing, spread, preferred_element_type=jnp.float32).astype(
            jnp.bfloat16
        )
        step = min(128, rows)

        def part(t, carry):
            at = pl.multiple_of(t * step, step)
            row = lax.broadcasted_iota(jnp.int32, (step, plane), 0) + at
            choose = (place(row) == lax.broadcasted_iota(jnp.int32, (step, plane), 1)).astype(
                jnp.bfloat16
            )
            full = jnp.dot(choose, right_part, preferred_element_type=jnp.float32)
            same = lax.rem(
                lax.broadcasted_iota(jnp.int32, (step, rows), 0), SUB
            ) == lax.rem(lax.broadcasted_iota(jnp.int32, (step, rows), 1), SUB)
            mi[pl.ds(at, step), :] = jnp.where(same, full, 0.0).astype(jnp.bfloat16)
            return carry

        lax.fori_loop(0, rows // step, part, 0)

    arrive(load_sem.at[0], in0)
    for copy in loads[0]:
        copy.wait()
    pl.semaphore_wait(barrier, 2 + (ny - 1) + (nz - 1))

    for s in range(SWEEPS):
        local_solve(s, 2)
        z_send(s, 3, sent.at[s, 2])
        if s == 0:
            for copy in loads[1] + loads[2] + tables:
                copy.wait()
        local_solve(s, 0)
        x_send(s, 0, left, 1)
        local_solve(s, 1)
        x_send(s, 1, right, 0)
        for g in ORDER[1:4]:
            local_solve(s, g ^ 1)
            z_send(s, g, sent.at[s, g ^ 1])
        if s == 0:
            build_mixing()
        for g in ORDER[4:]:
            arrive(xr_sem.at[s, g], xr.at[s, g])
            z_send(s, g, xr.at[s, g])
        for t in range(FACES + 2):
            if t < FACES:
                g = ORDER[t]
                arrive(r_sem.at[s, 0, g], zr.at[s, g])
                k_send(s, g)
            if 1 <= t <= FACES:
                g = ORDER[t - 1]
                arrive(r_sem.at[s, 1, g], kr.at[s, g])
                update(s, g)
                k_return(s, g)
            if t >= 2:
                g = ORDER[t - 2]
                arrive(r_sem.at[s, 2, g], zs.at[s, g])
                z_return(s, g)
        for g in ORDER:
            arrive(r_sem.at[s, 3, g], in0.at[g])

    for s in range(SWEEPS):
        for g in range(FACES):
            arrive(s_sem.at[s, 0, g], zr.at[s, g, pl.ds(0, ny - 1)])
            arrive(s_sem.at[s, 1, g], kr.at[s, g, pl.ds(0, nz - 1)])
            arrive(s_sem.at[s, 2, g], kr.at[s, g, pl.ds(0, nz - 1)])
            arrive(s_sem.at[s, 3, g], zr.at[s, g, pl.ds(0, ny - 1)])
        for slot in range(2):
            arrive(xs_sem.at[s, slot], xr.at[s, slot])


def on_device(nx, ny, nz, traces, sources, local_ops, plane_coupling, face_owner):
    slabs = traces.shape[4]
    columns = traces.shape[5]
    rows = 2 * slabs
    plane = ny * nz
    block = rows // ny
    bf16 = jnp.bfloat16
    hbm = pl.BlockSpec(memory_space=pltpu.HBM)
    vmem = pl.BlockSpec(memory_space=pltpu.VMEM)
    faces = (FACES, rows, W)
    out = pl.pallas_call(
        functools.partial(kernel, nx, ny, nz, slabs),
        out_shape=jax.ShapeDtypeStruct((2, slabs, columns), bf16),
        in_specs=[hbm] * 5,
        out_specs=vmem,
        scratch_shapes=[
            pltpu.VMEM(faces, bf16),
            pltpu.VMEM(faces, bf16),
            pltpu.VMEM((SWEEPS,) + faces, bf16),
            pltpu.VMEM((SWEEPS, 2, rows, W), bf16),
            pltpu.VMEM((SWEEPS, FACES, ny, block, W), bf16),
            pltpu.VMEM((SWEEPS, FACES, nz, ny, SUB, W), bf16),
            pltpu.VMEM((SWEEPS, FACES, nz, ny, SUB, W), bf16),
            pltpu.VMEM((SWEEPS, FACES, ny, block, W), bf16),
            pltpu.VMEM((2, columns, columns), bf16),
            pltpu.VMEM((2, slabs, columns), bf16),
            pltpu.VMEM((rows, rows), bf16),
            pltpu.VMEM((plane, plane), bf16),
            pltpu.VMEM((1, plane), jnp.int32),
            pltpu.SemaphoreType.DMA((9,)),
            pltpu.SemaphoreType.DMA((SWEEPS, 2)),
            pltpu.SemaphoreType.DMA((SWEEPS, 2)),
            pltpu.SemaphoreType.DMA((SWEEPS, 4, FACES)),
            pltpu.SemaphoreType.DMA((SWEEPS, 4, FACES)),
        ],
        compiler_params=pltpu.CompilerParams(
            collective_id=0, has_side_effects=True, vmem_limit_bytes=36 << 20
        ),
    )(
        pltpu.with_memory_space_constraint(traces.reshape(2, slabs, columns), pltpu.HBM),
        pltpu.with_memory_space_constraint(sources.reshape(2, slabs, columns), pltpu.HBM),
        pltpu.with_memory_space_constraint(local_ops.reshape(2, columns, columns), pltpu.HBM),
        pltpu.with_memory_space_constraint(plane_coupling.reshape(plane, plane), pltpu.HBM),
        pltpu.with_memory_space_constraint(face_owner.reshape(1, plane), pltpu.HBM),
    )
    return out.reshape(traces.shape)


def solution(mesh):
    placed = (
        P(None, "gx", "gy", "gz", None, None),
        P(None, "gx", "gy", "gz", None, None),
        P(None, "gx", "gy", "gz", None, None),
        P("gx", None, None),
        P("gx", None),
    )
    sizes = tuple(mesh.shape[axis] for axis in ("gx", "gy", "gz"))
    return jax.shard_map(
        functools.partial(on_device, *sizes),
        mesh=mesh,
        in_specs=placed,
        out_specs=P(None, "gx", "gy", "gz", None, None),
        check_vma=False,
    )
```

```python
import functools

import jax
import jax.numpy as jnp
from jax import lax
from jax.experimental import pallas as pl
from jax.experimental.pallas import tpu as pltpu
from jax.sharding import PartitionSpec as P

SWEEPS = 2
FACES = 6
W = 128
SUB = 16
ORDER = (3, 2, 5, 4, 0, 1)
SHIFT_Y = {2: 1, 3: -1}
SHIFT_Z = {4: 1, 5: -1}
MESH = pl.DeviceIdType.MESH


def kernel(
    nx, ny, nz, slabs,
    traces, sources, ops, coupling_hbm, owners_hbm, out,
    in0, in1, sent, xr, zr, kr, ur, zs, sv, bv, mi, coupling, owners,
    load_sem, xs_sem, xr_sem, s_sem, r_sem,
):
    i = lax.axis_index("gx")
    j = lax.axis_index("gy")
    k = lax.axis_index("gz")
    rows = 2 * slabs
    block = rows // ny
    plane = ny * nz
    incoming = (in0, in1)

    for c in range(2):
        for f in range(FACES):
            pltpu.make_async_copy(
                traces.at[c, :, pl.ds(f * W, W)],
                in0.at[f, pl.ds(c * slabs, slabs), :],
                load_sem.at[0],
            ).start()
    tables = [
        pltpu.make_async_copy(coupling_hbm, coupling, load_sem.at[7]),
        pltpu.make_async_copy(owners_hbm, owners, load_sem.at[8]),
    ]
    loads = []
    for n, columns in enumerate((pl.ds(2 * W, W), pl.ds(0, 2 * W), pl.ds(3 * W, 3 * W))):
        load = [
            pltpu.make_async_copy(ops.at[:, :, columns], sv.at[:, :, columns], load_sem.at[1 + 2 * n]),
            pltpu.make_async_copy(
                sources.at[:, :, columns], bv.at[:, :, columns], load_sem.at[2 + 2 * n]
            ),
        ]
        for copy in load:
            copy.start()
        loads.append(load)
    for copy in tables:
        copy.start()

    barrier = pltpu.get_barrier_semaphore()
    left = lax.rem(i + nx - 1, nx)
    right = lax.rem(i + 1, nx)
    for target in (left, right):
        pl.semaphore_signal(barrier, inc=1, device_id={"gx": target}, device_id_type=MESH)
    for d in range(1, ny):
        pl.semaphore_signal(
            barrier, inc=1, device_id={"gy": lax.rem(j + d, ny)}, device_id_type=MESH
        )
    for d in range(1, nz):
        pl.semaphore_signal(
            barrier, inc=1, device_id={"gz": lax.rem(k + d, nz)}, device_id_type=MESH
        )

    def local_solve(s, f):
        w = jnp.concatenate([sv[0, :, f * W:(f + 1) * W], sv[1, :, f * W:(f + 1) * W]], axis=1)
        step = min(256, slabs)
        source = incoming[s]

        def part(t, carry):
            at = pl.multiple_of(t * step, step)
            im_at = pl.multiple_of(slabs + t * step, step)
            re = jnp.concatenate([source[g, pl.ds(at, step), :] for g in range(FACES)], axis=1)
            im = jnp.concatenate([source[g, pl.ds(im_at, step), :] for g in range(FACES)], axis=1)
            p = jnp.dot(re, w, preferred_element_type=jnp.float32)
            q = jnp.dot(im, w, preferred_element_type=jnp.float32)
            b0 = bv[0, pl.ds(at, step), f * W:(f + 1) * W].astype(jnp.float32)
            b1 = bv[1, pl.ds(at, step), f * W:(f + 1) * W].astype(jnp.float32)
            sent[s, f, pl.ds(at, step), :] = (p[:, :W] - q[:, W:] + b0).astype(jnp.bfloat16)
            sent[s, f, pl.ds(im_at, step), :] = (p[:, W:] + q[:, :W] + b1).astype(jnp.bfloat16)
            return carry

        lax.fori_loop(0, slabs // step, part, 0)

    def ring(n, body, far_first=False):
        def step(t, carry):
            if far_first:
                t = n - t
            half = (t + 1) // 2
            odd = lax.rem(t, 2)
            body(odd * half + (1 - odd) * (n - half))
            return carry

        lax.fori_loop(1, n, step, 0)

    def z_send(s, g, face):
        slot = lax.rem(j + SHIFT_Y.get(g, 0) + ny, ny)

        def one(d):
            to = lax.rem(j + d, ny)
            pltpu.make_async_remote_copy(
                src_ref=face.at[pl.ds(pl.multiple_of(to * block, block), block), :],
                dst_ref=zr.at[s, g, slot],
                send_sem=s_sem.at[s, 0, g],
                recv_sem=r_sem.at[s, 0, g],
                device_id={"gy": to},
                device_id_type=MESH,
            ).start()

        ring(ny, one)
        pltpu.make_async_copy(
            face.at[pl.ds(pl.multiple_of(j * block, block), block), :],
            zr.at[s, g, slot],
            r_sem.at[s, 0, g],
        ).start()

    def k_send(s, g):
        slot = lax.rem(k + SHIFT_Z.get(g, 0) + nz, nz)

        def one(d):
            to = lax.rem(k + d, nz)
            pltpu.make_async_remote_copy(
                src_ref=zr.at[s, g, :, pl.ds(pl.multiple_of(to * SUB, SUB), SUB), :],
                dst_ref=kr.at[s, g, slot],
                send_sem=s_sem.at[s, 1, g],
                recv_sem=r_sem.at[s, 1, g],
                device_id={"gz": to},
                device_id_type=MESH,
            ).start()

        ring(nz, one)
        pltpu.make_async_copy(
            zr.at[s, g, :, pl.ds(pl.multiple_of(k * SUB, SUB), SUB), :],
            kr.at[s, g, slot],
            r_sem.at[s, 1, g],
        ).start()

    def update(s, g):
        step = min(256, rows)
        values = kr[s, g].reshape(rows, W)

        def part(t, carry):
            at = pl.multiple_of(t * step, step)
            slots = step // (ny * SUB)
            first = t * slots
            coupled = jnp.dot(mi[pl.ds(at, step), :], values, preferred_element_type=jnp.float32)
            mine = kr[s, g, pl.ds(first, slots)].reshape(step, W).astype(jnp.float32)
            ur[s, g, pl.ds(first, slots)] = (
                (mine - coupled).astype(jnp.bfloat16).reshape(slots, ny, SUB, W)
            )
            return carry

        lax.fori_loop(0, rows // step, part, 0)

    def k_return(s, g):
        mine = pl.ds(pl.multiple_of(k * SUB, SUB), SUB)

        def one(d):
            to = lax.rem(k + d, nz)
            pltpu.make_async_remote_copy(
                src_ref=ur.at[s, g, to],
                dst_ref=zs.at[s, g, :, mine, :],
                send_sem=s_sem.at[s, 2, g],
                recv_sem=r_sem.at[s, 2, g],
                device_id={"gz": to},
                device_id_type=MESH,
            ).start()

        ring(nz, one)
        pltpu.make_async_copy(
            ur.at[s, g, k], zs.at[s, g, :, mine, :], r_sem.at[s, 2, g]
        ).start()

    def z_return(s, g):
        if s == SWEEPS - 1:
            part = slabs // block
            rows_at = pl.multiple_of(lax.rem(j, part) * block, block)
            home = out.at[j // part, pl.ds(rows_at, block), g * W:(g + 1) * W]
        else:
            rows_at = pl.multiple_of(j * block, block)
            home = incoming[s + 1].at[g, pl.ds(rows_at, block), :]

        def one(d):
            to = lax.rem(j + d, ny)
            pltpu.make_async_remote_copy(
                src_ref=zs.at[s, g, to],
                dst_ref=home,
                send_sem=s_sem.at[s, 3, g],
                recv_sem=r_sem.at[s, 3, g],
                device_id={"gy": to},
                device_id_type=MESH,
            ).start()

        ring(ny, one, far_first=True)
        pltpu.make_async_copy(
            zs.at[s, g, j], home, r_sem.at[s, 3, g]
        ).start()

    def arrive(sem, ref):
        pltpu.make_async_copy(ref, ref, sem).wait()

    def x_send(s, f, to, slot):
        pltpu.make_async_remote_copy(
            src_ref=sent.at[s, f],
            dst_ref=xr.at[s, slot],
            send_sem=xs_sem.at[s, slot],
            recv_sem=xr_sem.at[s, slot],
            device_id={"gx": to},
            device_id_type=MESH,
        ).start()

    def build_mixing():
        owner = jnp.broadcast_to(owners[...], (plane, plane))
        pick = (owner == lax.broadcasted_iota(jnp.int32, (plane, plane), 0)).astype(jnp.bfloat16)
        mixing = lax.dot_general(
            coupling[...], pick, (((1,), (1,)), ((), ())), preferred_element_type=jnp.float32
        )
        mixing = mixing.astype(jnp.bfloat16)

        def place(index):
            point = index // SUB
            return lax.rem(point, ny) * nz + point // ny

        column = lax.broadcasted_iota(jnp.int32, (plane, rows), 1)
        spread = (lax.broadcasted_iota(jnp.int32, (plane, rows), 0) == place(column)).astype(
            jnp.bfloat16
        )
        right_part = jnp.dot(mixing, spread, preferred_element_type=jnp.float32).astype(
            jnp.bfloat16
        )
        step = min(128, rows)

        def part(t, carry):
            at = pl.multiple_of(t * step, step)
            row = lax.broadcasted_iota(jnp.int32, (step, plane), 0) + at
            choose = (place(row) == lax.broadcasted_iota(jnp.int32, (step, plane), 1)).astype(
                jnp.bfloat16
            )
            full = jnp.dot(choose, right_part, preferred_element_type=jnp.float32)
            same = lax.rem(
                lax.broadcasted_iota(jnp.int32, (step, rows), 0), SUB
            ) == lax.rem(lax.broadcasted_iota(jnp.int32, (step, rows), 1), SUB)
            mi[pl.ds(at, step), :] = jnp.where(same, full, 0.0).astype(jnp.bfloat16)
            return carry

        lax.fori_loop(0, rows // step, part, 0)

    arrive(load_sem.at[0], in0)
    for copy in loads[0]:
        copy.wait()
    for s in range(SWEEPS):
        local_solve(s, 2)
        if s == 0:
            pl.semaphore_wait(barrier, 2 + (ny - 1) + (nz - 1))
        z_send(s, 3, sent.at[s, 2])
        if s == 0:
            for copy in loads[1] + loads[2] + tables:
                copy.wait()
        local_solve(s, 0)
        x_send(s, 0, left, 1)
        local_solve(s, 1)
        x_send(s, 1, right, 0)
        for g in ORDER[1:4]:
            local_solve(s, g ^ 1)
            z_send(s, g, sent.at[s, g ^ 1])
        if s == 0:
            build_mixing()
        for g in ORDER[4:]:
            arrive(xr_sem.at[s, g], xr.at[s, g])
            z_send(s, g, xr.at[s, g])
        for t in range(FACES + 2):
            if t < FACES:
                g = ORDER[t]
                arrive(r_sem.at[s, 0, g], zr.at[s, g])
                k_send(s, g)
            if 1 <= t <= FACES:
                g = ORDER[t - 1]
                arrive(r_sem.at[s, 1, g], kr.at[s, g])
                update(s, g)
                k_return(s, g)
            if t >= 2:
                g = ORDER[t - 2]
                arrive(r_sem.at[s, 2, g], zs.at[s, g])
                z_return(s, g)
        for g in ORDER:
            arrive(r_sem.at[s, 3, g], in0.at[g])

    for s in range(SWEEPS):
        for g in range(FACES):
            arrive(s_sem.at[s, 0, g], zr.at[s, g, pl.ds(0, ny - 1)])
            arrive(s_sem.at[s, 1, g], kr.at[s, g, pl.ds(0, nz - 1)])
            arrive(s_sem.at[s, 2, g], kr.at[s, g, pl.ds(0, nz - 1)])
            arrive(s_sem.at[s, 3, g], zr.at[s, g, pl.ds(0, ny - 1)])
        for slot in range(2):
            arrive(xs_sem.at[s, slot], xr.at[s, slot])


def on_device(nx, ny, nz, traces, sources, local_ops, plane_coupling, face_owner):
    slabs = traces.shape[4]
    columns = traces.shape[5]
    rows = 2 * slabs
    plane = ny * nz
    block = rows // ny
    bf16 = jnp.bfloat16
    hbm = pl.BlockSpec(memory_space=pltpu.HBM)
    vmem = pl.BlockSpec(memory_space=pltpu.VMEM)
    faces = (FACES, rows, W)
    out = pl.pallas_call(
        functools.partial(kernel, nx, ny, nz, slabs),
        out_shape=jax.ShapeDtypeStruct((2, slabs, columns), bf16),
        in_specs=[hbm] * 5,
        out_specs=vmem,
        scratch_shapes=[
            pltpu.VMEM(faces, bf16),
            pltpu.VMEM(faces, bf16),
            pltpu.VMEM((SWEEPS,) + faces, bf16),
            pltpu.VMEM((SWEEPS, 2, rows, W), bf16),
            pltpu.VMEM((SWEEPS, FACES, ny, block, W), bf16),
            pltpu.VMEM((SWEEPS, FACES, nz, ny, SUB, W), bf16),
            pltpu.VMEM((SWEEPS, FACES, nz, ny, SUB, W), bf16),
            pltpu.VMEM((SWEEPS, FACES, ny, block, W), bf16),
            pltpu.VMEM((2, columns, columns), bf16),
            pltpu.VMEM((2, slabs, columns), bf16),
            pltpu.VMEM((rows, rows), bf16),
            pltpu.VMEM((plane, plane), bf16),
            pltpu.VMEM((1, plane), jnp.int32),
            pltpu.SemaphoreType.DMA((9,)),
            pltpu.SemaphoreType.DMA((SWEEPS, 2)),
            pltpu.SemaphoreType.DMA((SWEEPS, 2)),
            pltpu.SemaphoreType.DMA((SWEEPS, 4, FACES)),
            pltpu.SemaphoreType.DMA((SWEEPS, 4, FACES)),
        ],
        compiler_params=pltpu.CompilerParams(
            collective_id=0, has_side_effects=True, vmem_limit_bytes=36 << 20
        ),
    )(
        pltpu.with_memory_space_constraint(traces.reshape(2, slabs, columns), pltpu.HBM),
        pltpu.with_memory_space_constraint(sources.reshape(2, slabs, columns), pltpu.HBM),
        pltpu.with_memory_space_constraint(local_ops.reshape(2, columns, columns), pltpu.HBM),
        pltpu.with_memory_space_constraint(plane_coupling.reshape(plane, plane), pltpu.HBM),
        pltpu.with_memory_space_constraint(face_owner.reshape(1, plane), pltpu.HBM),
    )
    return out.reshape(traces.shape)


def solution(mesh):
    placed = (
        P(None, "gx", "gy", "gz", None, None),
        P(None, "gx", "gy", "gz", None, None),
        P(None, "gx", "gy", "gz", None, None),
        P("gx", None, None),
        P("gx", None),
    )
    sizes = tuple(mesh.shape[axis] for axis in ("gx", "gy", "gz"))
    return jax.shard_map(
        functools.partial(on_device, *sizes),
        mesh=mesh,
        in_specs=placed,
        out_specs=P(None, "gx", "gy", "gz", None, None),
        check_vma=False,
    )
```

```python
import functools

import jax
import jax.numpy as jnp
from jax import lax
from jax.experimental import pallas as pl
from jax.experimental.pallas import tpu as pltpu
from jax.sharding import PartitionSpec as P

SWEEPS = 2
FACES = 6
W = 128
SUB = 16
ORDER = (3, 2, 5, 4, 0, 1)
KORDER = (4, 1, 5, 3, 7, 2, 6)
SHIFT_Y = {2: 1, 3: -1}
SHIFT_Z = {4: 1, 5: -1}
MESH = pl.DeviceIdType.MESH


def kernel(
    nx, ny, nz, slabs,
    traces, sources, ops, coupling_hbm, owners_hbm, out,
    in0, in1, sent, xr, zr, kr, ur, zs, sv, bv, mi, coupling, owners,
    load_sem, xs_sem, xr_sem, s_sem, r_sem,
):
    i = lax.axis_index("gx")
    j = lax.axis_index("gy")
    k = lax.axis_index("gz")
    rows = 2 * slabs
    block = rows // ny
    plane = ny * nz
    incoming = (in0, in1)

    for c in range(2):
        for f in range(FACES):
            pltpu.make_async_copy(
                traces.at[c, :, pl.ds(f * W, W)],
                in0.at[f, pl.ds(c * slabs, slabs), :],
                load_sem.at[0],
            ).start()
    tables = [
        pltpu.make_async_copy(coupling_hbm, coupling, load_sem.at[7]),
        pltpu.make_async_copy(owners_hbm, owners, load_sem.at[8]),
    ]
    loads = []
    for n, columns in enumerate((pl.ds(2 * W, W), pl.ds(0, 2 * W), pl.ds(3 * W, 3 * W))):
        load = [
            pltpu.make_async_copy(ops.at[:, :, columns], sv.at[:, :, columns], load_sem.at[1 + 2 * n]),
            pltpu.make_async_copy(
                sources.at[:, :, columns], bv.at[:, :, columns], load_sem.at[2 + 2 * n]
            ),
        ]
        for copy in load:
            copy.start()
        loads.append(load)
    for copy in tables:
        copy.start()

    barrier = pltpu.get_barrier_semaphore()
    left = lax.rem(i + nx - 1, nx)
    right = lax.rem(i + 1, nx)
    for target in (left, right):
        pl.semaphore_signal(barrier, inc=1, device_id={"gx": target}, device_id_type=MESH)
    for d in range(1, ny):
        pl.semaphore_signal(
            barrier, inc=1, device_id={"gy": lax.rem(j + d, ny)}, device_id_type=MESH
        )
    for d in range(1, nz):
        pl.semaphore_signal(
            barrier, inc=1, device_id={"gz": lax.rem(k + d, nz)}, device_id_type=MESH
        )

    def local_solve(s, f):
        w = jnp.concatenate([sv[0, :, f * W:(f + 1) * W], sv[1, :, f * W:(f + 1) * W]], axis=1)
        step = min(256, slabs)
        source = incoming[s]

        def part(t, carry):
            at = pl.multiple_of(t * step, step)
            im_at = pl.multiple_of(slabs + t * step, step)
            re = jnp.concatenate([source[g, pl.ds(at, step), :] for g in range(FACES)], axis=1)
            im = jnp.concatenate([source[g, pl.ds(im_at, step), :] for g in range(FACES)], axis=1)
            p = jnp.dot(re, w, preferred_element_type=jnp.float32)
            q = jnp.dot(im, w, preferred_element_type=jnp.float32)
            b0 = bv[0, pl.ds(at, step), f * W:(f + 1) * W].astype(jnp.float32)
            b1 = bv[1, pl.ds(at, step), f * W:(f + 1) * W].astype(jnp.float32)
            sent[s, f, pl.ds(at, step), :] = (p[:, :W] - q[:, W:] + b0).astype(jnp.bfloat16)
            sent[s, f, pl.ds(im_at, step), :] = (p[:, W:] + q[:, :W] + b1).astype(jnp.bfloat16)
            return carry

        lax.fori_loop(0, slabs // step, part, 0)

    def ring(n, body, far_first=False):
        def step(t, carry):
            if far_first:
                t = n - t
            half = (t + 1) // 2
            odd = lax.rem(t, 2)
            body(odd * half + (1 - odd) * (n - half))
            return carry

        lax.fori_loop(1, n, step, 0)

    def z_send(s, g, face):
        slot = lax.rem(j + SHIFT_Y.get(g, 0) + ny, ny)

        def one(d):
            to = lax.rem(j + d, ny)
            pltpu.make_async_remote_copy(
                src_ref=face.at[pl.ds(pl.multiple_of(to * block, block), block), :],
                dst_ref=zr.at[s, g, slot],
                send_sem=s_sem.at[s, 0, g],
                recv_sem=r_sem.at[s, 0, g],
                device_id={"gy": to},
                device_id_type=MESH,
            ).start()

        ring(ny, one)
        pltpu.make_async_copy(
            face.at[pl.ds(pl.multiple_of(j * block, block), block), :],
            zr.at[s, g, slot],
            r_sem.at[s, 0, g],
        ).start()

    def k_send(s, g):
        slot = lax.rem(k + SHIFT_Z.get(g, 0) + nz, nz)

        def one(d):
            to = lax.rem(k + d, nz)
            pltpu.make_async_remote_copy(
                src_ref=zr.at[s, g, :, pl.ds(pl.multiple_of(to * SUB, SUB), SUB), :],
                dst_ref=kr.at[s, g, slot],
                send_sem=s_sem.at[s, 1, g],
                recv_sem=r_sem.at[s, 1, g],
                device_id={"gz": to},
                device_id_type=MESH,
            ).start()

        for d in KORDER if nz == 8 else range(1, nz):
            one(d)
        pltpu.make_async_copy(
            zr.at[s, g, :, pl.ds(pl.multiple_of(k * SUB, SUB), SUB), :],
            kr.at[s, g, slot],
            r_sem.at[s, 1, g],
        ).start()

    def update(s, g):
        step = min(256, rows)
        values = kr[s, g].reshape(rows, W)

        def part(t, carry):
            at = pl.multiple_of(t * step, step)
            slots = step // (ny * SUB)
            first = t * slots
            coupled = jnp.dot(mi[pl.ds(at, step), :], values, preferred_element_type=jnp.float32)
            mine = kr[s, g, pl.ds(first, slots)].reshape(step, W).astype(jnp.float32)
            ur[s, g, pl.ds(first, slots)] = (
                (mine - coupled).astype(jnp.bfloat16).reshape(slots, ny, SUB, W)
            )
            return carry

        lax.fori_loop(0, rows // step, part, 0)

    def k_return(s, g):
        mine = pl.ds(pl.multiple_of(k * SUB, SUB), SUB)

        def one(d):
            to = lax.rem(k + d, nz)
            pltpu.make_async_remote_copy(
                src_ref=ur.at[s, g, to],
                dst_ref=zs.at[s, g, :, mine, :],
                send_sem=s_sem.at[s, 2, g],
                recv_sem=r_sem.at[s, 2, g],
                device_id={"gz": to},
                device_id_type=MESH,
            ).start()

        for d in KORDER if nz == 8 else range(1, nz):
            one(d)
        pltpu.make_async_copy(
            ur.at[s, g, k], zs.at[s, g, :, mine, :], r_sem.at[s, 2, g]
        ).start()

    def z_return(s, g):
        if s == SWEEPS - 1:
            part = slabs // block
            rows_at = pl.multiple_of(lax.rem(j, part) * block, block)
            home = out.at[j // part, pl.ds(rows_at, block), g * W:(g + 1) * W]
        else:
            rows_at = pl.multiple_of(j * block, block)
            home = incoming[s + 1].at[g, pl.ds(rows_at, block), :]

        def one(d):
            to = lax.rem(j + d, ny)
            pltpu.make_async_remote_copy(
                src_ref=zs.at[s, g, to],
                dst_ref=home,
                send_sem=s_sem.at[s, 3, g],
                recv_sem=r_sem.at[s, 3, g],
                device_id={"gy": to},
                device_id_type=MESH,
            ).start()

        ring(ny, one, far_first=True)
        pltpu.make_async_copy(
            zs.at[s, g, j], home, r_sem.at[s, 3, g]
        ).start()

    def arrive(sem, ref):
        pltpu.make_async_copy(ref, ref, sem).wait()

    def x_send(s, f, to, slot):
        pltpu.make_async_remote_copy(
            src_ref=sent.at[s, f],
            dst_ref=xr.at[s, slot],
            send_sem=xs_sem.at[s, slot],
            recv_sem=xr_sem.at[s, slot],
            device_id={"gx": to},
            device_id_type=MESH,
        ).start()

    def build_mixing():
        owner = jnp.broadcast_to(owners[...], (plane, plane))
        pick = (owner == lax.broadcasted_iota(jnp.int32, (plane, plane), 0)).astype(jnp.bfloat16)
        mixing = lax.dot_general(
            coupling[...], pick, (((1,), (1,)), ((), ())), preferred_element_type=jnp.float32
        )
        mixing = mixing.astype(jnp.bfloat16)

        def place(index):
            point = index // SUB
            return lax.rem(point, ny) * nz + point // ny

        column = lax.broadcasted_iota(jnp.int32, (plane, rows), 1)
        spread = (lax.broadcasted_iota(jnp.int32, (plane, rows), 0) == place(column)).astype(
            jnp.bfloat16
        )
        right_part = jnp.dot(mixing, spread, preferred_element_type=jnp.float32).astype(
            jnp.bfloat16
        )
        step = min(128, rows)

        def part(t, carry):
            at = pl.multiple_of(t * step, step)
            row = lax.broadcasted_iota(jnp.int32, (step, plane), 0) + at
            choose = (place(row) == lax.broadcasted_iota(jnp.int32, (step, plane), 1)).astype(
                jnp.bfloat16
            )
            full = jnp.dot(choose, right_part, preferred_element_type=jnp.float32)
            same = lax.rem(
                lax.broadcasted_iota(jnp.int32, (step, rows), 0), SUB
            ) == lax.rem(lax.broadcasted_iota(jnp.int32, (step, rows), 1), SUB)
            mi[pl.ds(at, step), :] = jnp.where(same, full, 0.0).astype(jnp.bfloat16)
            return carry

        lax.fori_loop(0, rows // step, part, 0)

    arrive(load_sem.at[0], in0)
    for copy in loads[0]:
        copy.wait()
    for s in range(SWEEPS):
        local_solve(s, 2)
        if s == 0:
            pl.semaphore_wait(barrier, 2 + (ny - 1) + (nz - 1))
        z_send(s, 3, sent.at[s, 2])
        if s == 0:
            for copy in loads[1] + loads[2] + tables:
                copy.wait()
        local_solve(s, 0)
        x_send(s, 0, left, 1)
        local_solve(s, 1)
        x_send(s, 1, right, 0)
        for g in ORDER[1:4]:
            local_solve(s, g ^ 1)
            z_send(s, g, sent.at[s, g ^ 1])
        if s == 0:
            build_mixing()
        for g in ORDER[4:]:
            arrive(xr_sem.at[s, g], xr.at[s, g])
            z_send(s, g, xr.at[s, g])
        for t in range(FACES + 2):
            if t < FACES:
                g = ORDER[t]
                arrive(r_sem.at[s, 0, g], zr.at[s, g])
                k_send(s, g)
            if 1 <= t <= FACES:
                g = ORDER[t - 1]
                arrive(r_sem.at[s, 1, g], kr.at[s, g])
                update(s, g)
                k_return(s, g)
            if t >= 2:
                g = ORDER[t - 2]
                arrive(r_sem.at[s, 2, g], zs.at[s, g])
                z_return(s, g)
        for g in ORDER:
            arrive(r_sem.at[s, 3, g], in0.at[g])

    for s in range(SWEEPS):
        for g in range(FACES):
            arrive(s_sem.at[s, 0, g], zr.at[s, g, pl.ds(0, ny - 1)])
            arrive(s_sem.at[s, 1, g], kr.at[s, g, pl.ds(0, nz - 1)])
            arrive(s_sem.at[s, 2, g], kr.at[s, g, pl.ds(0, nz - 1)])
            arrive(s_sem.at[s, 3, g], zr.at[s, g, pl.ds(0, ny - 1)])
        for slot in range(2):
            arrive(xs_sem.at[s, slot], xr.at[s, slot])


def on_device(nx, ny, nz, traces, sources, local_ops, plane_coupling, face_owner):
    slabs = traces.shape[4]
    columns = traces.shape[5]
    rows = 2 * slabs
    plane = ny * nz
    block = rows // ny
    bf16 = jnp.bfloat16
    hbm = pl.BlockSpec(memory_space=pltpu.HBM)
    vmem = pl.BlockSpec(memory_space=pltpu.VMEM)
    faces = (FACES, rows, W)
    out = pl.pallas_call(
        functools.partial(kernel, nx, ny, nz, slabs),
        out_shape=jax.ShapeDtypeStruct((2, slabs, columns), bf16),
        in_specs=[hbm] * 5,
        out_specs=vmem,
        scratch_shapes=[
            pltpu.VMEM(faces, bf16),
            pltpu.VMEM(faces, bf16),
            pltpu.VMEM((SWEEPS,) + faces, bf16),
            pltpu.VMEM((SWEEPS, 2, rows, W), bf16),
            pltpu.VMEM((SWEEPS, FACES, ny, block, W), bf16),
            pltpu.VMEM((SWEEPS, FACES, nz, ny, SUB, W), bf16),
            pltpu.VMEM((SWEEPS, FACES, nz, ny, SUB, W), bf16),
            pltpu.VMEM((SWEEPS, FACES, ny, block, W), bf16),
            pltpu.VMEM((2, columns, columns), bf16),
            pltpu.VMEM((2, slabs, columns), bf16),
            pltpu.VMEM((rows, rows), bf16),
            pltpu.VMEM((plane, plane), bf16),
            pltpu.VMEM((1, plane), jnp.int32),
            pltpu.SemaphoreType.DMA((9,)),
            pltpu.SemaphoreType.DMA((SWEEPS, 2)),
            pltpu.SemaphoreType.DMA((SWEEPS, 2)),
            pltpu.SemaphoreType.DMA((SWEEPS, 4, FACES)),
            pltpu.SemaphoreType.DMA((SWEEPS, 4, FACES)),
        ],
        compiler_params=pltpu.CompilerParams(
            collective_id=0, has_side_effects=True, vmem_limit_bytes=36 << 20
        ),
    )(
        pltpu.with_memory_space_constraint(traces.reshape(2, slabs, columns), pltpu.HBM),
        pltpu.with_memory_space_constraint(sources.reshape(2, slabs, columns), pltpu.HBM),
        pltpu.with_memory_space_constraint(local_ops.reshape(2, columns, columns), pltpu.HBM),
        pltpu.with_memory_space_constraint(plane_coupling.reshape(plane, plane), pltpu.HBM),
        pltpu.with_memory_space_constraint(face_owner.reshape(1, plane), pltpu.HBM),
    )
    return out.reshape(traces.shape)


def solution(mesh):
    placed = (
        P(None, "gx", "gy", "gz", None, None),
        P(None, "gx", "gy", "gz", None, None),
        P(None, "gx", "gy", "gz", None, None),
        P("gx", None, None),
        P("gx", None),
    )
    sizes = tuple(mesh.shape[axis] for axis in ("gx", "gy", "gz"))
    return jax.shard_map(
        functools.partial(on_device, *sizes),
        mesh=mesh,
        in_specs=placed,
        out_specs=P(None, "gx", "gy", "gz", None, None),
        check_vma=False,
    )
```
